32 devices in a mesh: rep: 4 (over x, core), dom: 8 (over z, y).
Axes of the slice: x: 2, y: 2, z: 4, core: 2. Of those that a mesh axis runs over, the one named last changes fastest.
Arguments:
- coords: float32 [4, 3, 32768], P('rep', None, 'dom'), may hold values from -6 to 6
- atom_var: float32 [32768], P('dom'), may hold values from 0.2 to 1
- atom_weight: float32 [32768], P('dom'), may hold values from 0.5 to 2
- atoms_live: int32 [256], P('dom'), may hold values from 1 to 128, 24576 in all
- block_list: int32 [256, 16], P('dom'), may hold values from 0 to 2047, as said below
- owner_map: int32 [2048], replicated, may hold values from 0 to 2047, as said below
- comp_means: float32 [3, 262144], replicated, may hold values from -6 to 6
- comp_var: float32 [262144], replicated, may hold values from 0.3 to 1.5
- comp_weight: float32 [262144], replicated, may hold values from 0.1 to 1
- target: float32 [262144], P('dom'), may hold values from 0 to 2
- noise_sigma: float32 [262144], P('dom'), may hold values from 0.05 to 0.5
Outputs:
- intersection_avg: float32 [262144], P('dom')
- forces: float32 [4, 3, 32768], P('rep', None, 'dom')
The draws below stay inside these ranges and needn't reach their ends.
Inputs may be any that keep to these rules, and one draw needn't show every extreme that they name: `atoms_live`: entry a is the number of live atoms of atom block a, held in the first slots of the block. `owner_map`: A permutation of the component blocks. Storage position p lies on dom index p // 256. `block_list`: of the 32 x 16 entries of one dom index's atom blocks, at most 64 name blocks whose storage position lies on any one dom index, and in every draw some dom index receives exactly 64 entries from every dom index. An atom block may list a component block more than once; each entry counts.
All inputs are finite; a program needn't handle non-finite values.
Results may differ from the reference program's by a relative error of at most 0.0003.
Values sent between devices are 32-bit elements; how exact they have to be, the bound alone decides.
A program may use at most 128 MiB of HBM per device.

```python
import math
import jax
import jax.numpy as jnp
import numpy as np
from jax import lax

NCOMP = 262144
ATOM_BLK = 128
COMP_BLK = 128
LISTED = 16
REPLICAS = 4
ATOMS = 32768
BLK_DEV = 32
ATOM_BLOCKS = 256
COMP_BLOCKS = 2048
CAPACITY = 64
N_DOM = 8


def owner_table(key):
    return jax.random.permutation(jax.random.fold_in(key, 11), COMP_BLOCKS).astype(jnp.int32)


def draw_owner_map(key, part):
    return owner_table(key)


def draw_block_list(key, part):
    perm = owner_table(key)
    inverse = jnp.zeros((COMP_BLOCKS,), jnp.int32).at[perm].set(jnp.arange(COMP_BLOCKS, dtype=jnp.int32))
    per_owner = COMP_BLOCKS // N_DOM
    entries = BLK_DEV * LISTED
    base = jax.random.fold_in(key, 23)
    hottest = jax.random.randint(jax.random.fold_in(base, 1), (), 0, N_DOM).astype(jnp.int32)

    def one_domain(domain_key):
        first, second, third = jax.random.split(domain_key, 3)
        pool = jax.random.permutation(first, (N_DOM - 1) * CAPACITY)[:entries - CAPACITY].astype(jnp.int32)
        others = (hottest + 1 + pool // CAPACITY) % N_DOM
        chosen = jnp.concatenate([jnp.full((CAPACITY,), hottest, jnp.int32), others])
        chosen = jax.random.permutation(second, chosen)
        inside = jax.random.randint(third, (entries,), 0, per_owner).astype(jnp.int32)
        return inverse[chosen * per_owner + inside].reshape(BLK_DEV, LISTED)
    domain_keys = jax.random.split(jax.random.fold_in(base, 2), N_DOM)
    return jax.vmap(one_domain)(domain_keys).reshape(BLK_DEV * N_DOM, LISTED).astype(jnp.int32)


def shard_levels(stream_key, dims, shards, low, high):
    def one(axis_at, blocks):
        draws = jax.random.uniform(jax.random.fold_in(jax.random.fold_in(stream_key, 6), axis_at), (blocks,), jnp.float32, low / len(shards), high / len(shards))
        return jnp.repeat(jnp.exp(draws), dims[axis_at] // blocks).reshape((-1,) + (1,) * (len(dims) - axis_at - 1))

    level = one(*shards[0])
    for cut in shards[1:]:
        level = level * one(*cut)
    return level


def split_up(count, total, reach, lean):
    loads = [(1 << 20) // math.isqrt(grade ** lean) + 1 for grade in range(2, count + 1)]
    spare, given = total - reach - (count - 1), [1] * (count - 1)
    while spare > 0:
        free = [i for i in range(count - 1) if given[i] < reach]
        mass, left = sum([loads[i] for i in free]), spare
        for i in free:
            more = min(reach - given[i], max(1, left * loads[i] // mass), spare)
            given[i] = given[i] + more
            spare = spare - more
    return np.array([reach] + given)


def uneven_parts(rng, number_of, total, limit, skew):
    if number_of == 2:
        one = jax.random.randint(rng, (), max(1, total - limit), min(limit, total - 1) + 1)
        return jnp.stack([one, total - one])
    tallies = jnp.asarray(split_up(number_of, total, limit, skew), jnp.int32)
    pairs = (number_of - 1) // 2
    source_of, receiver = tallies[1:1 + 2 * pairs:2], tallies[2:2 + 2 * pairs:2]
    room = jnp.minimum(source_of - 1, limit - receiver)
    passed = jax.random.randint(jax.random.fold_in(rng, 1), (pairs,), 0, 1 << 20) % (room + 1)
    tallies = tallies.at[1:1 + 2 * pairs:2].set(source_of - passed).at[2:2 + 2 * pairs:2].set(receiver + passed)
    return tallies[jax.random.permutation(jax.random.fold_in(rng, 2), number_of)]


def normal_values(key, dims, deviation, bound, pieces=(), held_as=jnp.bfloat16):
    drawn = deviation * jax.random.normal(key, dims, jnp.float32)
    if pieces:
        drawn = drawn * shard_levels(key, dims, pieces, -0.22, 0.18)
    return jnp.clip(drawn, -bound, bound).astype(held_as)


def setup_inputs(seed: int = 0) -> dict:
    key_list = jax.random.split(jax.random.key(seed), 12)
    return {
        "coords": normal_values(key_list[0], (REPLICAS, 3, ATOMS), 1.0, 6.0, ((0, 4), (2, 8)), jnp.float32),
        "atom_var": jnp.clip(jnp.exp(math.log(1.0) - 1.609438 * jax.random.uniform(key_list[1], (ATOMS,), jnp.float32) ** shard_levels(key_list[1], (ATOMS,), ((0, 8),), -0.2, 0.2)), 0.2, 1.0),
        "atom_weight": jnp.clip(0.5 + 1.5 * jax.random.uniform(key_list[2], (ATOMS,), jnp.float32) ** shard_levels(key_list[2], (ATOMS,), ((0, 8),), -0.2, 0.2), 0.5, 2.0),
        "atoms_live": uneven_parts(key_list[3], ATOM_BLOCKS, ATOM_BLOCKS * ATOM_BLK * 3 // 4, ATOM_BLK, 0).astype(jnp.int32),
        "block_list": draw_block_list(jax.random.fold_in(key_list[11], 71), 0),
        "owner_map": draw_owner_map(jax.random.fold_in(key_list[11], 71), 0),
        "comp_means": normal_values(key_list[6], (3, NCOMP), 1.0, 6.0, (), jnp.float32),
        "comp_var": jnp.clip(jnp.exp(jax.random.uniform(key_list[7], (NCOMP,), jnp.float32, math.log(0.3), math.log(1.5))), 0.3, 1.5),
        "comp_weight": jnp.clip(jnp.exp(jax.random.uniform(key_list[8], (NCOMP,), jnp.float32, math.log(0.1), math.log(1.0))), 0.1, 1.0),
        "target": jnp.clip(2.0 * jax.random.uniform(key_list[9], (NCOMP,), jnp.float32) ** shard_levels(key_list[9], (NCOMP,), ((0, 8),), -0.2, 0.2), 0.0, 2.0),
        "noise_sigma": jnp.clip(jnp.exp(math.log(0.5) - 2.3025851 * jax.random.uniform(key_list[10], (NCOMP,), jnp.float32) ** shard_levels(key_list[10], (NCOMP,), ((0, 8),), -0.2, 0.2)), 0.05, 0.5),
    }


full_turn = 2.0 * math.pi
energy_unit = 2.494


def intersection_tile(positions, variances, weights, centers, center_var, center_weight):
    offsets = positions[:, None, :, None] - centers[:, :, None, :]
    squared = jnp.sum(offsets * offsets, axis=0)
    widths = variances[None, :, None] + center_var[:, None, :]
    prefactor = weights[None, :, None] * center_weight[:, None, :]
    intersection = prefactor * (full_turn * widths) ** -1.5 * jnp.exp(-0.5 * squared / widths)
    return offsets, widths, intersection


def reference(coords, atom_var, atom_weight, atoms_live, block_list, owner_map, comp_means, comp_var, comp_weight, target, noise_sigma):
    blocks = block_list.shape[0]
    replicas = coords.shape[0]
    slot_index = jnp.arange(ATOM_BLK, dtype=jnp.int32)
    live_mask = (slot_index[None, :] < atoms_live[:, None]).astype(atom_weight.dtype)
    positions = coords.reshape(replicas, 3, blocks, ATOM_BLK).transpose(2, 0, 1, 3)
    variances = atom_var.reshape(blocks, ATOM_BLK)
    weights = atom_weight.reshape(blocks, ATOM_BLK) * live_mask
    centers = comp_means.reshape(3, COMP_BLOCKS, COMP_BLK)
    center_var = comp_var.reshape(COMP_BLOCKS, COMP_BLK)
    center_weight = comp_weight.reshape(COMP_BLOCKS, COMP_BLK)
    tiled = jax.vmap(intersection_tile, in_axes=(0, None, None, None, None, None))

    def partial_of(inputs):
        coord_tile, var_tile, weight_tile, blocks_of = inputs
        offsets, widths, intersection = tiled(coord_tile, var_tile, weight_tile, centers[:, blocks_of], center_var[blocks_of], center_weight[blocks_of])
        return jnp.sum(intersection, axis=2)

    inputs = (positions, variances, weights, block_list)
    partials = lax.map(partial_of, inputs)
    flattened = partials.transpose(0, 2, 1, 3).reshape(blocks * LISTED, replicas, COMP_BLK)
    summed = jax.ops.segment_sum(flattened, block_list.reshape(-1), num_segments=COMP_BLOCKS)
    mean_logical = jnp.sum(summed, axis=1) / replicas
    intersection_avg = jnp.zeros_like(mean_logical).at[owner_map].set(mean_logical).reshape(-1)
    wanted = target.reshape(COMP_BLOCKS, COMP_BLK)[owner_map]
    sigmas = noise_sigma.reshape(COMP_BLOCKS, COMP_BLK)[owner_map]
    misfit = mean_logical - wanted
    adjoint = misfit / (sigmas * sigmas + 0.5 * misfit * misfit) / replicas

    def force_of(inputs):
        coord_tile, var_tile, weight_tile, blocks_of = inputs
        offsets, widths, intersection = tiled(coord_tile, var_tile, weight_tile, centers[:, blocks_of], center_var[blocks_of], center_weight[blocks_of])
        weight = adjoint[blocks_of][None, :, None, :] * (intersection / widths)
        return energy_unit * jnp.sum(weight[:, None] * offsets, axis=(2, 4))

    forces = lax.map(force_of, inputs)
    forces = forces.transpose(1, 2, 0, 3).reshape(replicas, 3, blocks * ATOM_BLK)
    return intersection_avg, forces
```

```python
import functools
import math

import jax
import jax.numpy as jnp
from jax import lax
from jax.experimental import pallas as pl
from jax.experimental.pallas import tpu as pltpu
from jax.sharding import PartitionSpec as P

CAPACITY = 64
ROWS = CAPACITY + 8
LANES = 128
SUB = 32

energy_unit = 2.494
norm = (2.0 * math.pi) ** -1.5
half_log2e = -0.5 / math.log(2.0)
VMEM = pltpu.VMEM
MESH = pl.DeviceIdType.MESH


def three(value):
    first = value.astype(jnp.bfloat16)
    rest = value - first.astype(jnp.float32)
    second = rest.astype(jnp.bfloat16)
    third = (rest - second.astype(jnp.float32)).astype(jnp.bfloat16)
    return first, second, third


def three_f32(value):
    return [piece.astype(jnp.float32) for piece in three(value)]


def pair_kernel(
    listed, owned, live, lst, owner, x_ref, av_ref, aw_ref, m_ref, cv_ref, cw_ref,
    send_ref, pos_ref, g_ref, count, avb, wb,
):
    a = pl.program_id(0)
    domains = send_ref.shape[0]

    @pl.when(a == 0)
    def _():
        send_ref[...] = jnp.zeros_like(send_ref)
        send_ref[:, CAPACITY : CAPACITY + 8, :] = jnp.full((domains, 8, LANES), -1.0, jnp.float32)
        for d in range(domains):
            count[d] = 0

    x = x_ref[...]
    lane = lax.broadcasted_iota(jnp.int32, (1, LANES), 1)
    weights = jnp.where(lane < live[a], aw_ref[0], 0.0)
    avb[...] = jnp.transpose(jnp.broadcast_to(av_ref[0], (LANES, LANES)))
    wb[...] = jnp.transpose(jnp.broadcast_to(weights, (LANES, LANES)))
    xx = jnp.sum(x * x, axis=0, keepdims=True)
    left = half_log2e * jnp.concatenate(
        [-2.0 * x, jnp.ones((1, LANES), jnp.float32), xx, jnp.zeros((3, LANES), jnp.float32)], axis=0
    )
    l0, l1, l2 = three_f32(left)
    lhs = jnp.concatenate([l0, l0, l1, l1, l0, l2], axis=0).astype(jnp.bfloat16)
    for k in range(listed):
        b = lst[a * listed + k]
        m = m_ref[:, pl.ds(pl.multiple_of(b * LANES, LANES), LANES)]
        mm = jnp.sum(m * m, axis=0, keepdims=True)
        right = jnp.concatenate(
            [m, mm, jnp.ones((1, LANES), jnp.float32), jnp.zeros((3, LANES), jnp.float32)], axis=0
        )
        r0, r1, r2 = three_f32(right)
        rhs = jnp.concatenate([r0, r1, r0, r1, r2, r0], axis=0).astype(jnp.bfloat16)
        scaled = lax.dot_general(
            lhs, rhs, (((0,), (0,)), ((), ())), preferred_element_type=jnp.float32
        )
        cv = cv_ref[pl.ds(b, 1), :]
        total = jnp.zeros((SUB, LANES), jnp.float32)
        for h in range(LANES // SUB):
            rows = slice(h * SUB, (h + 1) * SUB)
            root = lax.rsqrt(avb[rows, :] + cv)
            inv = root * root
            ov = (root * inv) * jnp.exp2(scaled[rows] * inv) * wb[rows, :]
            g_ref[k * LANES + h * SUB : k * LANES + (h + 1) * SUB, :] = ov * inv
            total = total + ov
        partial = jnp.sum(total, axis=0, keepdims=True) * (norm * cw_ref[pl.ds(b, 1), :])
        place = owner[b]
        dev = lax.div(place, owned)
        slot = place - dev * owned
        rank = count[dev]
        count[dev] = rank + 1
        pos_ref[a * listed + k] = dev * CAPACITY + rank
        send_ref[dev, pl.ds(rank, 1), :] = partial
        before = send_ref[dev, CAPACITY : CAPACITY + 1, :]
        send_ref[dev, CAPACITY : CAPACITY + 1, :] = jnp.where(
            lane == rank, slot.astype(jnp.float32), before
        )


def force_kernel(listed, pos, lst, x_ref, g_ref, ret_ref, m_ref, cw_ref, f_ref, coef, sums):
    a = pl.program_id(0)
    for k in range(listed):
        b = lst[a * listed + k]
        adj = ret_ref[pl.ds(pos[a * listed + k], 1), :]
        scale = adj * (cw_ref[pl.ds(b, 1), :] * (energy_unit * norm))
        m = m_ref[:, pl.ds(pl.multiple_of(b * LANES, LANES), LANES)]
        coef[k, 0] = jnp.broadcast_to(scale, (8, LANES))
        for c in range(3):
            coef[k, c + 1] = jnp.broadcast_to(scale * m[c : c + 1], (8, LANES))
    step = 16
    for h in range(LANES // step):
        acc = [jnp.zeros((step // 8, 8, LANES), jnp.float32) for _ in range(4)]
        for k in range(listed):
            g = g_ref[k * LANES + h * step : k * LANES + (h + 1) * step, :].reshape(
                step // 8, 8, LANES
            )
            for c in range(4):
                acc[c] = acc[c] + g * coef[k, c][None]
        for c in range(4):
            sums[c, h * step : (h + 1) * step, :] = acc[c].reshape(step, LANES)
    ones = jnp.ones((8, LANES), jnp.float32)
    flat = [
        lax.dot_general(
            ones, sums[c], (((1,), (1,)), ((), ())), precision=lax.Precision.HIGHEST,
            preferred_element_type=jnp.float32,
        )[0:1]
        for c in range(4)
    ]
    for c in range(3):
        f_ref[c : c + 1, :] = x_ref[c : c + 1, :] * flat[0] - flat[c + 1]


def exchange_kernel(
    domains, replicas, send_ref, target_ref, sigma_ref, mean_ref, ret_ref,
    got, acc, part, back, land, out_send, out_recv, rep_send, rep_recv, back_send, back_recv,
):
    me_d = lax.axis_index("dom")
    me_r = lax.axis_index("rep")
    owned = target_ref.shape[0]
    stages = replicas.bit_length() - 1
    partners = []
    for t in range(stages):
        bit = 1 << t
        partners.append(me_r + bit - 2 * bit * lax.rem(lax.div(me_r, bit), 2))
    barrier = pltpu.get_barrier_semaphore()
    for s in range(1, domains):
        pl.semaphore_signal(
            barrier, inc=1, device_id=(me_r, lax.rem(me_d + s, domains)), device_id_type=MESH
        )
    for t in range(stages):
        pl.semaphore_signal(barrier, inc=1, device_id=(partners[t], me_d), device_id_type=MESH)
    pl.semaphore_wait(barrier, domains - 1 + stages)

    outs = [None]
    for s in range(1, domains):
        peer = lax.rem(me_d + s, domains)
        copy = pltpu.make_async_remote_copy(
            src_ref=send_ref.at[peer],
            dst_ref=got.at[s],
            send_sem=out_send.at[s],
            recv_sem=out_recv.at[s],
            device_id=(me_r, peer),
            device_id_type=MESH,
        )
        copy.start()
        outs.append(copy)

    row = lax.broadcasted_iota(jnp.int32, (owned, CAPACITY), 0).astype(jnp.float32)

    def picks_of(s):
        slots = (
            send_ref[me_d, CAPACITY : CAPACITY + 1, :] if s == 0 else got[s, CAPACITY : CAPACITY + 1, :]
        )
        return jnp.where(row == slots[:, :CAPACITY], 1.0, 0.0).astype(jnp.bfloat16)

    total = jnp.zeros((owned, LANES), jnp.float32)
    for s in range(domains):
        if s:
            outs[s].wait_recv()
        rows = send_ref[me_d, :CAPACITY, :] if s == 0 else got[s, :CAPACITY, :]
        picks = picks_of(s)
        for piece in three(rows):
            total = total + jnp.dot(picks, piece, preferred_element_type=jnp.float32)
    acc[0] = total
    swaps = []
    for t in range(stages):
        copy = pltpu.make_async_remote_copy(
            src_ref=acc.at[t],
            dst_ref=part.at[t],
            send_sem=rep_send.at[t],
            recv_sem=rep_recv.at[t],
            device_id=(partners[t], me_d),
            device_id_type=MESH,
        )
        copy.start()
        swaps.append(copy)
        copy.wait_recv()
        total = total + part[t]
        if t + 1 < stages:
            acc[t + 1] = total
    mean = total / replicas
    mean_ref[...] = mean
    misfit = mean - target_ref[...]
    sigmas = sigma_ref[...]
    adjoint = misfit / (sigmas * sigmas + 0.5 * misfit * misfit) / replicas
    pieces = three(adjoint)
    backs = []
    for s in list(range(1, domains)) + [0]:
        picks = picks_of(s)
        rows = jnp.zeros((CAPACITY, LANES), jnp.float32)
        for piece in pieces:
            rows = rows + lax.dot_general(
                picks, piece, (((0,), (0,)), ((), ())), preferred_element_type=jnp.float32
            )
        if s == 0:
            ret_ref[me_d] = rows
            continue
        back[s] = rows
        peer = lax.rem(me_d + domains - s, domains)
        copy = pltpu.make_async_remote_copy(
            src_ref=back.at[s],
            dst_ref=land.at[s],
            send_sem=back_send.at[s],
            recv_sem=back_recv.at[s],
            device_id=(me_r, peer),
            device_id_type=MESH,
        )
        copy.start()
        backs.append((s, copy))
    for s, copy in backs:
        copy.wait_recv()
        ret_ref[lax.rem(me_d + s, domains)] = land[s]
    for copy in outs[1:] + swaps + [copy for _, copy in backs]:
        copy.wait_send()


def shards(
    coords, atom_var, atom_weight, atoms_live, block_list, owner_map,
    comp_means, comp_var, comp_weight, target, noise_sigma,
):
    replicas = lax.axis_size("rep")
    domains = lax.axis_size("dom")
    blocks, listed = block_list.shape
    comp_blocks = owner_map.shape[0]
    owned = target.shape[0] // LANES
    entries = blocks * listed
    x = coords[0]
    lst = block_list.reshape(-1)
    cv = comp_var.reshape(comp_blocks, LANES)
    cw = comp_weight.reshape(comp_blocks, LANES)
    whole = pl.BlockSpec(memory_space=VMEM)
    per_block = pl.BlockSpec((1, 1, LANES), lambda a, *_: (a, 0, 0))
    x_spec = pl.BlockSpec((3, LANES), lambda a, *_: (0, a))
    g_spec = pl.BlockSpec((listed * LANES, LANES), lambda a, *_: (a, 0))
    send, pos, g = pl.pallas_call(
        functools.partial(pair_kernel, listed, owned),
        grid_spec=pltpu.PrefetchScalarGridSpec(
            num_scalar_prefetch=3,
            grid=(blocks,),
            in_specs=[x_spec, per_block, per_block, whole, whole, whole],
            out_specs=[whole, pl.BlockSpec(memory_space=pltpu.SMEM), g_spec],
            scratch_shapes=[
                pltpu.SMEM((domains,), jnp.int32),
                VMEM((LANES, LANES), jnp.float32),
                VMEM((LANES, LANES), jnp.float32),
            ],
        ),
        out_shape=[
            jax.ShapeDtypeStruct((domains, ROWS, LANES), jnp.float32),
            jax.ShapeDtypeStruct((entries,), jnp.int32),
            jax.ShapeDtypeStruct((entries * LANES, LANES), jnp.float32),
        ],
        compiler_params=pltpu.CompilerParams(vmem_limit_bytes=40 << 20),
        name="pairs",
    )(
        atoms_live, lst, owner_map, x,
        atom_var.reshape(blocks, 1, LANES), atom_weight.reshape(blocks, 1, LANES),
        comp_means, cv, cw,
    )
    stages = replicas.bit_length() - 1
    mean, ret = pl.pallas_call(
        functools.partial(exchange_kernel, domains, replicas),
        in_specs=[whole] * 3,
        out_specs=[whole] * 2,
        out_shape=[
            jax.ShapeDtypeStruct((owned, LANES), jnp.float32),
            jax.ShapeDtypeStruct((domains, CAPACITY, LANES), jnp.float32),
        ],
        scratch_shapes=[
            VMEM((domains, ROWS, LANES), jnp.float32),
            VMEM((stages, owned, LANES), jnp.float32),
            VMEM((stages, owned, LANES), jnp.float32),
            VMEM((domains, CAPACITY, LANES), jnp.float32),
            VMEM((domains, CAPACITY, LANES), jnp.float32),
            pltpu.SemaphoreType.DMA((domains,)),
            pltpu.SemaphoreType.DMA((domains,)),
            pltpu.SemaphoreType.DMA((stages,)),
            pltpu.SemaphoreType.DMA((stages,)),
            pltpu.SemaphoreType.DMA((domains,)),
            pltpu.SemaphoreType.DMA((domains,)),
        ],
        compiler_params=pltpu.CompilerParams(
            collective_id=0, has_side_effects=True, vmem_limit_bytes=24 << 20
        ),
        name="exchange",
    )(send, target.reshape(owned, LANES), noise_sigma.reshape(owned, LANES))
    forces = pl.pallas_call(
        functools.partial(force_kernel, listed),
        grid_spec=pltpu.PrefetchScalarGridSpec(
            num_scalar_prefetch=2,
            grid=(blocks,),
            in_specs=[x_spec, g_spec, whole, whole, whole],
            out_specs=x_spec,
            scratch_shapes=[
                VMEM((listed, 4, 8, LANES), jnp.float32),
                VMEM((4, LANES, LANES), jnp.float32),
            ],
        ),
        out_shape=jax.ShapeDtypeStruct((3, blocks * LANES), jnp.float32),
        compiler_params=pltpu.CompilerParams(vmem_limit_bytes=40 << 20),
        name="forces",
    )(pos, lst, x, g, ret.reshape(domains * CAPACITY, LANES), comp_means, cw)
    return (mean.reshape(-1), forces[None])


def solution(mesh):
    return jax.shard_map(
        shards,
        mesh=mesh,
        in_specs=(
            P("rep", None, "dom"),
            P("dom"),
            P("dom"),
            P("dom"),
            P("dom", None),
            P(),
            P(),
            P(),
            P(),
            P("dom"),
            P("dom"),
        ),
        out_specs=(P("dom"), P("rep", None, "dom")),
        check_vma=False,
    )
```

```python
import functools
import math

import jax
import jax.numpy as jnp
from jax import lax
from jax.experimental import pallas as pl
from jax.experimental.pallas import tpu as pltpu
from jax.sharding import PartitionSpec as P

CAPACITY = 64
ROWS = CAPACITY + 8
LANES = 128
SUB = 32
OUT_SLOTS = 3
IN_SLOTS = 5

energy_unit = 2.494
norm = (2.0 * math.pi) ** -1.5
half_log2e = -0.5 / math.log(2.0)
VMEM = pltpu.VMEM
MESH = pl.DeviceIdType.MESH


def three(value):
    first = value.astype(jnp.bfloat16)
    rest = value - first.astype(jnp.float32)
    second = rest.astype(jnp.bfloat16)
    third = (rest - second.astype(jnp.float32)).astype(jnp.bfloat16)
    return first, second, third


def three_f32(value):
    return [piece.astype(jnp.float32) for piece in three(value)]


def pair_kernel(
    listed, owned, live_h, lst_h, owner_h, x_h, av_h, aw_h, m_h, cv_h, cw_h,
    send_ref, pos_ref, table_ref, g_h,
    g_buf, g_sems, live, lst, owner, x_v, av_v, aw_v, m_v, cv_v, cw_v, count, avb, wb, lhs_s, rhs_s, cvs, sums, sems,
):
    domains = send_ref.shape[0]
    blocks = live.shape[0]
    loads = [
        pltpu.make_async_copy(src, dst, sems.at[i])
        for i, (src, dst) in enumerate(
            [(m_h, m_v), (cv_h, cv_v), (cw_h, cw_v), (x_h, x_v), (av_h, av_v), (aw_h, aw_v),
             (owner_h, owner), (lst_h, lst), (live_h, live)]
        )
    ]
    for load in loads:
        load.start()
    send_ref[...] = jnp.zeros_like(send_ref)
    send_ref[:, CAPACITY : CAPACITY + 8, :] = jnp.full((domains, 8, LANES), -1.0, jnp.float32)
    for d in range(domains):
        count[d] = 0
    for load in loads:
        load.wait()
    lane = lax.broadcasted_iota(jnp.int32, (1, LANES), 1)
    one = jnp.ones((1, LANES), jnp.float32)
    none = jnp.zeros((3, LANES), jnp.float32)

    def out_copy(a, h):
        turn = lax.rem(a, OUT_SLOTS)
        return pltpu.make_async_copy(g_buf.at[turn, h], g_h.at[a, h], g_sems.at[turn, h])

    def drain(a):
        for h in range(LANES // SUB):

            @pl.when(live[a] > h * SUB)
            def _():
                out_copy(a, h).wait()

    def block(a, carry):
        n_live = live[a]
        turn = lax.rem(a, OUT_SLOTS)

        @pl.when(a >= OUT_SLOTS)
        def _():
            drain(a - OUT_SLOTS)

        x = jnp.concatenate(
            [x_v[c, :, pl.ds(pl.multiple_of(a * LANES, LANES), LANES)] for c in range(3)], axis=0
        )
        weights = jnp.where(lane < n_live, aw_v[pl.ds(a, 1), :], 0.0)
        avb[...] = jnp.transpose(jnp.broadcast_to(av_v[pl.ds(a, 1), :], (LANES, LANES)))
        wb[...] = jnp.transpose(jnp.broadcast_to(weights, (LANES, LANES)))
        xx = jnp.sum(x * x, axis=0, keepdims=True)
        left = half_log2e * jnp.concatenate([-2.0 * x, one, xx, none], axis=0)
        l0, l1, l2 = three_f32(left)
        pad = jnp.zeros((LANES - 48, LANES), jnp.float32)
        lhs_s[...] = jnp.transpose(jnp.concatenate([l0, l0, l1, l1, l0, l2, pad], axis=0)).astype(
            jnp.bfloat16
        )
        for k in range(listed):
            e = a * listed + k
            b = lst[e]
            m = m_v[:, pl.ds(pl.multiple_of(b * LANES, LANES), LANES)]
            mm = jnp.sum(m * m, axis=0, keepdims=True)
            r0, r1, r2 = three_f32(jnp.concatenate([m, mm, one, none], axis=0))
            rhs_s[:, k * LANES : (k + 1) * LANES] = jnp.concatenate(
                [r0, r1, r0, r1, r2, r0], axis=0
            ).astype(jnp.bfloat16)
            cvs[k] = jnp.broadcast_to(cv_v[pl.ds(b, 1), :], (8, LANES))
            scale = norm * cw_v[pl.ds(b, 1), :]
            table_ref[e] = scale * jnp.concatenate([one, m], axis=0)
            sums[k] = jnp.zeros((8, LANES), jnp.float32)
        for h in range(LANES // SUB):

            @pl.when(n_live > h * SUB)
            def _():
                left_rows = lhs_s[h * SUB : (h + 1) * SUB, :48]
                for k in range(0, listed, 2):
                    both = jnp.dot(
                        left_rows, rhs_s[:, k * LANES : (k + 2) * LANES],
                        preferred_element_type=jnp.float32,
                    )
                    for n in range(2):
                        total = sums[k + n]
                        cv = cvs[k + n]
                        for q in range(0, SUB, 8):
                            rows = slice(h * SUB + q, h * SUB + q + 8)
                            root = lax.rsqrt(avb[rows, :] + cv)
                            inv = root * root
                            ex = jnp.exp2(both[q : q + 8, n * LANES : (n + 1) * LANES] * inv)
                            ov = (root * inv) * (ex * wb[rows, :])
                            g_buf[turn, h, (k + n) * SUB + q : (k + n) * SUB + q + 8, :] = ov * inv
                            total = total + ov
                        sums[k + n] = total
                out_copy(a, h).start()

        for k in range(listed):
            e = a * listed + k
            partial = jnp.sum(sums[k], axis=0, keepdims=True) * table_ref[e][0:1]
            place = owner[lst[e]]
            dev = lax.div(place, owned)
            slot = place - dev * owned
            rank = count[dev]
            count[dev] = rank + 1
            pos_ref[e] = dev * CAPACITY + rank
            send_ref[dev, pl.ds(rank, 1), :] = partial
            before = send_ref[dev, CAPACITY : CAPACITY + 1, :]
            send_ref[dev, CAPACITY : CAPACITY + 1, :] = jnp.where(
                lane == rank, slot.astype(jnp.float32), before
            )
        return carry

    lax.fori_loop(0, blocks, block, 0)
    for last in range(max(0, blocks - OUT_SLOTS), blocks):
        drain(last)


def force_kernel(
    listed, pos_h, live_h, x_h, g_h, ret_ref, table_ref, mean_v, f_ref, mean_h,
    g_buf, g_sems, pos, live, x_v, coef, sums, sems,
):
    blocks = live.shape[0]
    loads = [
        pltpu.make_async_copy(src, dst, sems.at[i])
        for i, (src, dst) in enumerate([(pos_h, pos), (live_h, live), (x_h, x_v), (mean_v, mean_h)])
    ]
    for load in loads:
        load.start()
    for load in loads[:3]:
        load.wait()
    ones = jnp.ones((8, LANES), jnp.float32)

    def in_copy(a, h):
        turn = lax.rem(a, IN_SLOTS)
        return pltpu.make_async_copy(g_h.at[a, h], g_buf.at[turn, h], g_sems.at[turn, h])

    def fetch(a):
        for h in range(LANES // SUB):

            @pl.when(live[a] > h * SUB)
            def _():
                in_copy(a, h).start()

    for first in range(min(IN_SLOTS - 1, blocks)):
        fetch(first)

    def block(a, carry):
        n_live = live[a]
        turn = lax.rem(a, IN_SLOTS)

        @pl.when(a + IN_SLOTS - 1 < blocks)
        def _():
            fetch(a + IN_SLOTS - 1)

        for k in range(listed):
            e = a * listed + k
            scale = energy_unit * ret_ref[pl.ds(pos[e], 1), :]
            rows = table_ref[e] * scale
            for c in range(4):
                coef[k, c] = jnp.broadcast_to(rows[c : c + 1], (8, LANES))
        for h in range(LANES // SUB):

            @pl.when(n_live > h * SUB)
            def _():
                in_copy(a, h).wait()
                acc = [[jnp.zeros((8, LANES), jnp.float32) for _ in range(SUB // 8)] for _ in range(4)]
                for k in range(listed):
                    for q in range(SUB // 8):
                        g = g_buf[turn, h, k * SUB + q * 8 : k * SUB + q * 8 + 8, :]
                        for c in range(4):
                            acc[c][q] = acc[c][q] + g * coef[k, c]
                for c in range(4):
                    for q in range(SUB // 8):
                        sums[c, h * SUB + q * 8 : h * SUB + q * 8 + 8, :] = acc[c][q]

            @pl.when(n_live <= h * SUB)
            def _():
                sums[:, h * SUB : (h + 1) * SUB, :] = jnp.zeros((4, SUB, LANES), jnp.float32)

        flat = [
            lax.dot_general(
                ones, sums[c], (((1,), (1,)), ((), ())), precision=lax.Precision.HIGHEST,
                preferred_element_type=jnp.float32,
            )[0:1]
            for c in range(4)
        ]
        here = pl.ds(pl.multiple_of(a * LANES, LANES), LANES)
        for c in range(3):
            f_ref[c, :, here] = x_v[c, :, here] * flat[0] - flat[c + 1]
        return carry

    lax.fori_loop(0, blocks, block, 0)
    loads[3].wait()


def exchange_kernel(
    domains, replicas, send_ref, target_h, sigma_h, mean_ref, ret_ref,
    target_ref, sigma_ref, loads, got, acc, part, back, land, out_send, out_recv, rep_send, rep_recv, back_send, back_recv,
):
    me_d = lax.axis_index("dom")
    me_r = lax.axis_index("rep")
    owned = target_ref.shape[0]
    stages = replicas.bit_length() - 1
    partners = []
    for t in range(stages):
        bit = 1 << t
        partners.append(me_r + bit - 2 * bit * lax.rem(lax.div(me_r, bit), 2))
    fetches = [
        pltpu.make_async_copy(target_h, target_ref, loads.at[0]),
        pltpu.make_async_copy(sigma_h, sigma_ref, loads.at[1]),
    ]
    for fetch in fetches:
        fetch.start()
    barrier = pltpu.get_barrier_semaphore()
    for s in range(1, domains):
        pl.semaphore_signal(
            barrier, inc=1, device_id=(me_r, lax.rem(me_d + s, domains)), device_id_type=MESH
        )
    for t in range(stages):
        pl.semaphore_signal(barrier, inc=1, device_id=(partners[t], me_d), device_id_type=MESH)
    pl.semaphore_wait(barrier, domains - 1 + stages)

    outs = [None]
    for s in range(1, domains):
        peer = lax.rem(me_d + s, domains)
        copy = pltpu.make_async_remote_copy(
            src_ref=send_ref.at[peer],
            dst_ref=got.at[s],
            send_sem=out_send.at[s],
            recv_sem=out_recv.at[s],
            device_id=(me_r, peer),
            device_id_type=MESH,
        )
        copy.start()
        outs.append(copy)

    row = lax.broadcasted_iota(jnp.int32, (owned, CAPACITY), 0).astype(jnp.float32)

    def picks_of(s):
        slots = (
            send_ref[me_d, CAPACITY : CAPACITY + 1, :] if s == 0 else got[s, CAPACITY : CAPACITY + 1, :]
        )
        return jnp.where(row == slots[:, :CAPACITY], 1.0, 0.0).astype(jnp.bfloat16)

    total = jnp.zeros((owned, LANES), jnp.float32)
    for s in range(domains):
        if s:
            outs[s].wait_recv()
        rows = send_ref[me_d, :CAPACITY, :] if s == 0 else got[s, :CAPACITY, :]
        picks = picks_of(s)
        for piece in three(rows):
            total = total + jnp.dot(picks, piece, preferred_element_type=jnp.float32)
    acc[0] = total
    swaps = []
    for t in range(stages):
        copy = pltpu.make_async_remote_copy(
            src_ref=acc.at[t],
            dst_ref=part.at[t],
            send_sem=rep_send.at[t],
            recv_sem=rep_recv.at[t],
            device_id=(partners[t], me_d),
            device_id_type=MESH,
        )
        copy.start()
        swaps.append(copy)
        copy.wait_recv()
        total = total + part[t]
        if t + 1 < stages:
            acc[t + 1] = total
    mean = total / replicas
    mean_ref[...] = mean
    for fetch in fetches:
        fetch.wait()
    misfit = mean - target_ref[...]
    sigmas = sigma_ref[...]
    adjoint = misfit / (sigmas * sigmas + 0.5 * misfit * misfit) / replicas
    pieces = three(adjoint)
    backs = []
    for s in list(range(1, domains)) + [0]:
        picks = picks_of(s)
        rows = jnp.zeros((CAPACITY, LANES), jnp.float32)
        for piece in pieces:
            rows = rows + lax.dot_general(
                picks, piece, (((0,), (0,)), ((), ())), preferred_element_type=jnp.float32
            )
        if s == 0:
            ret_ref[me_d] = rows
            continue
        back[s] = rows
        peer = lax.rem(me_d + domains - s, domains)
        copy = pltpu.make_async_remote_copy(
            src_ref=back.at[s],
            dst_ref=land.at[s],
            send_sem=back_send.at[s],
            recv_sem=back_recv.at[s],
            device_id=(me_r, peer),
            device_id_type=MESH,
        )
        copy.start()
        backs.append((s, copy))
    for s, copy in backs:
        copy.wait_recv()
        ret_ref[lax.rem(me_d + s, domains)] = land[s]
    for copy in outs[1:] + swaps + [copy for _, copy in backs]:
        copy.wait_send()


def shards(
    coords, atom_var, atom_weight, atoms_live, block_list, owner_map,
    comp_means, comp_var, comp_weight, target, noise_sigma,
):
    replicas = lax.axis_size("rep")
    domains = lax.axis_size("dom")
    blocks, listed = block_list.shape
    comp_blocks = owner_map.shape[0]
    owned = target.shape[0] // LANES
    entries = blocks * listed
    x = coords.transpose(1, 0, 2)
    lst = block_list.reshape(-1)
    cv = comp_var.reshape(comp_blocks, LANES)
    cw = comp_weight.reshape(comp_blocks, LANES)
    f32, i32, bf16 = jnp.float32, jnp.int32, jnp.bfloat16
    whole = pl.BlockSpec(memory_space=VMEM)
    far = pl.BlockSpec(memory_space=pltpu.HBM)
    send, pos, table, g = pl.pallas_call(
        functools.partial(pair_kernel, listed, owned),
        in_specs=[far] * 9,
        out_specs=[whole, pl.BlockSpec(memory_space=pltpu.SMEM), whole, far],
        out_shape=[
            jax.ShapeDtypeStruct((domains, ROWS, LANES), f32),
            jax.ShapeDtypeStruct((entries,), i32),
            jax.ShapeDtypeStruct((entries, 4, LANES), f32),
            jax.ShapeDtypeStruct((blocks, LANES // SUB, listed * SUB, LANES), f32),
        ],
        scratch_shapes=[
            VMEM((OUT_SLOTS, LANES // SUB, listed * SUB, LANES), f32),
            pltpu.SemaphoreType.DMA((OUT_SLOTS, LANES // SUB)),
            pltpu.SMEM((blocks,), i32),
            pltpu.SMEM((entries,), i32),
            pltpu.SMEM((comp_blocks,), i32),
            VMEM(x.shape, f32),
            VMEM((blocks, LANES), f32),
            VMEM((blocks, LANES), f32),
            VMEM(comp_means.shape, f32),
            VMEM(cv.shape, f32),
            VMEM(cw.shape, f32),
            pltpu.SMEM((domains,), i32),
            VMEM((LANES, LANES), f32),
            VMEM((LANES, LANES), f32),
            VMEM((LANES, LANES), bf16),
            VMEM((48, listed * LANES), bf16),
            VMEM((listed, 8, LANES), f32),
            VMEM((listed, 8, LANES), f32),
            pltpu.SemaphoreType.DMA((9,)),
        ],
        compiler_params=pltpu.CompilerParams(vmem_limit_bytes=57 << 20),
        name="pairs",
    )(
        atoms_live, lst, owner_map, x,
        atom_var.reshape(blocks, LANES), atom_weight.reshape(blocks, LANES),
        comp_means, cv, cw,
    )
    stages = replicas.bit_length() - 1
    mean, ret = pl.pallas_call(
        functools.partial(exchange_kernel, domains, replicas),
        in_specs=[whole, far, far],
        out_specs=[whole] * 2,
        out_shape=[
            jax.ShapeDtypeStruct((owned, LANES), f32),
            jax.ShapeDtypeStruct((domains, CAPACITY, LANES), f32),
        ],
        scratch_shapes=[
            VMEM((owned, LANES), f32),
            VMEM((owned, LANES), f32),
            pltpu.SemaphoreType.DMA((2,)),
            VMEM((domains, ROWS, LANES), f32),
            VMEM((stages, owned, LANES), f32),
            VMEM((stages, owned, LANES), f32),
            VMEM((domains, CAPACITY, LANES), f32),
            VMEM((domains, CAPACITY, LANES), f32),
            pltpu.SemaphoreType.DMA((domains,)),
            pltpu.SemaphoreType.DMA((domains,)),
            pltpu.SemaphoreType.DMA((stages,)),
            pltpu.SemaphoreType.DMA((stages,)),
            pltpu.SemaphoreType.DMA((domains,)),
            pltpu.SemaphoreType.DMA((domains,)),
        ],
        compiler_params=pltpu.CompilerParams(
            collective_id=0, has_side_effects=True, vmem_limit_bytes=57 << 20
        ),
        name="exchange",
    )(send, target.reshape(owned, LANES), noise_sigma.reshape(owned, LANES))
    forces, mean = pl.pallas_call(
        functools.partial(force_kernel, listed),
        in_specs=[pl.BlockSpec(memory_space=pl.ANY), far, far, far, whole, whole, whole],
        out_specs=[whole, far],
        out_shape=[
            jax.ShapeDtypeStruct(x.shape, f32),
            jax.ShapeDtypeStruct((owned, LANES), f32),
        ],
        scratch_shapes=[
            VMEM((IN_SLOTS, LANES // SUB, listed * SUB, LANES), f32),
            pltpu.SemaphoreType.DMA((IN_SLOTS, LANES // SUB)),
            pltpu.SMEM((entries,), i32),
            pltpu.SMEM((blocks,), i32),
            VMEM(x.shape, f32),
            VMEM((listed, 4, 8, LANES), f32),
            VMEM((4, LANES, LANES), f32),
            pltpu.SemaphoreType.DMA((4,)),
        ],
        compiler_params=pltpu.CompilerParams(vmem_limit_bytes=57 << 20),
        name="forces",
    )(pos, atoms_live, x, g, ret.reshape(domains * CAPACITY, LANES), table, mean)
    return (mean.reshape(-1), forces.transpose(1, 0, 2))


def solution(mesh):
    return jax.shard_map(
        shards,
        mesh=mesh,
        in_specs=(
            P("rep", None, "dom"),
            P("dom"),
            P("dom"),
            P("dom"),
            P("dom", None),
            P(),
            P(),
            P(),
            P(),
            P("dom"),
            P("dom"),
        ),
        out_specs=(P("dom"), P("rep", None, "dom")),
        check_vma=False,
    )
```

```python
import functools
import math

import jax
import jax.numpy as jnp
from jax import lax
from jax.experimental import pallas as pl
from jax.experimental.pallas import tpu as pltpu
from jax.sharding import PartitionSpec as P

CAPACITY = 64
ROWS = CAPACITY + 8
LANES = 128
SUB = 32
HALF = 16
OUT_SLOTS = 3
IN_SLOTS = 5

energy_unit = 2.494
norm = (2.0 * math.pi) ** -1.5
half_log2e = -0.5 / math.log(2.0)
VMEM = pltpu.VMEM
MESH = pl.DeviceIdType.MESH


def three(value):
    first = value.astype(jnp.bfloat16)
    rest = value - first.astype(jnp.float32)
    second = rest.astype(jnp.bfloat16)
    third = (rest - second.astype(jnp.float32)).astype(jnp.bfloat16)
    return first, second, third


def three_f32(value):
    return [piece.astype(jnp.float32) for piece in three(value)]


def pair_kernel(
    listed, owned, live_h, lst_h, owner_h, x_h, av_h, aw_h, m_h, cv_h, cw_h,
    send_ref, pos_ref, table_ref, g_h,
    g_buf, g_sems, live, lst, owner, x_v, av_v, aw_v, m_v, cv_v, cw_v, count, avb, wb, sems,
):
    domains = send_ref.shape[0]
    blocks = live.shape[0]
    loads = [
        pltpu.make_async_copy(src, dst, sems.at[i])
        for i, (src, dst) in enumerate(
            [(m_h, m_v), (cv_h, cv_v), (cw_h, cw_v), (x_h, x_v), (av_h, av_v), (aw_h, aw_v),
             (owner_h, owner), (lst_h, lst), (live_h, live)]
        )
    ]
    for load in loads:
        load.start()
    send_ref[...] = jnp.zeros_like(send_ref)
    send_ref[:, CAPACITY : CAPACITY + 8, :] = jnp.full((domains, 8, LANES), -1.0, jnp.float32)
    for d in range(domains):
        count[d] = 0
    for load in loads:
        load.wait()
    lane = lax.broadcasted_iota(jnp.int32, (1, LANES), 1)
    one = jnp.ones((1, LANES), jnp.float32)
    none = jnp.zeros((3, LANES), jnp.float32)

    def out_copy(a):
        turn = lax.rem(a, OUT_SLOTS)
        return pltpu.make_async_copy(g_buf.at[turn], g_h.at[a], g_sems.at[turn])

    def block(a, carry):
        turn = lax.rem(a, OUT_SLOTS)

        @pl.when(a >= OUT_SLOTS)
        def _():
            out_copy(a - OUT_SLOTS).wait()

        x = jnp.concatenate(
            [x_v[c, :, pl.ds(pl.multiple_of(a * LANES, LANES), LANES)] for c in range(3)], axis=0
        )
        weights = jnp.where(lane < live[a], aw_v[pl.ds(a, 1), :], 0.0)
        avb[...] = jnp.transpose(jnp.broadcast_to(av_v[pl.ds(a, 1), :], (LANES, LANES)))
        wb[...] = jnp.transpose(jnp.broadcast_to(weights, (LANES, LANES)))
        xx = jnp.sum(x * x, axis=0, keepdims=True)
        left = half_log2e * jnp.concatenate([-2.0 * x, one, xx, none], axis=0)
        l0, l1, l2 = three_f32(left)
        lhs = jnp.concatenate([l0, l0, l1, l1, l0, l2], axis=0).astype(jnp.bfloat16)
        for k in range(listed):
            e = a * listed + k
            b = lst[e]
            m = m_v[:, pl.ds(pl.multiple_of(b * LANES, LANES), LANES)]
            mm = jnp.sum(m * m, axis=0, keepdims=True)
            r0, r1, r2 = three_f32(jnp.concatenate([m, mm, one, none], axis=0))
            rhs = jnp.concatenate([r0, r1, r0, r1, r2, r0], axis=0).astype(jnp.bfloat16)
            scaled = lax.dot_general(
                lhs, rhs, (((0,), (0,)), ((), ())), preferred_element_type=jnp.float32
            )
            cv = cv_v[pl.ds(b, 1), :]
            total = jnp.zeros((SUB, LANES), jnp.float32)
            for h in range(LANES // SUB):
                rows = slice(h * SUB, (h + 1) * SUB)
                root = lax.rsqrt(avb[rows, :] + cv)
                inv = root * root
                ov = (root * inv) * jnp.exp2(scaled[rows] * inv) * wb[rows, :]
                g_buf[turn, k * LANES + h * SUB : k * LANES + (h + 1) * SUB, :] = ov * inv
                total = total + ov
            scale = norm * cw_v[pl.ds(b, 1), :]
            table_ref[e] = scale * jnp.concatenate([one, m], axis=0)
            partial = jnp.sum(total, axis=0, keepdims=True) * scale
            place = owner[b]
            dev = lax.div(place, owned)
            slot = place - dev * owned
            rank = count[dev]
            count[dev] = rank + 1
            pos_ref[e] = dev * CAPACITY + rank
            send_ref[dev, pl.ds(rank, 1), :] = partial
            before = send_ref[dev, CAPACITY : CAPACITY + 1, :]
            send_ref[dev, CAPACITY : CAPACITY + 1, :] = jnp.where(
                lane == rank, slot.astype(jnp.float32), before
            )
        out_copy(a).start()
        return carry

    lax.fori_loop(0, blocks, block, 0)
    for last in range(max(0, blocks - OUT_SLOTS), blocks):
        out_copy(last).wait()


def force_kernel(
    listed, pos_h, x_h, g_h, ret_ref, table_ref, mean_v, f_ref, mean_h,
    g_buf, g_sems, pos, x_v, coef, sums, sems,
):
    blocks = x_v.shape[2] // LANES
    loads = [
        pltpu.make_async_copy(src, dst, sems.at[i])
        for i, (src, dst) in enumerate([(pos_h, pos), (x_h, x_v), (mean_v, mean_h)])
    ]
    for load in loads:
        load.start()
    for load in loads[:2]:
        load.wait()
    ones = jnp.ones((8, LANES), jnp.float32)

    def in_copy(a):
        turn = lax.rem(a, IN_SLOTS)
        return pltpu.make_async_copy(g_h.at[a], g_buf.at[turn], g_sems.at[turn])

    for first in range(min(IN_SLOTS - 1, blocks)):
        in_copy(first).start()

    def block(a, carry):
        turn = lax.rem(a, IN_SLOTS)

        @pl.when(a + IN_SLOTS - 1 < blocks)
        def _():
            in_copy(a + IN_SLOTS - 1).start()

        in_copy(a).wait()
        for k in range(listed):
            e = a * listed + k
            scale = energy_unit * ret_ref[pl.ds(pos[e], 1), :]
            rows = table_ref[e] * scale
            for c in range(4):
                coef[k, c] = jnp.broadcast_to(rows[c : c + 1], (8, LANES))
        for h in range(LANES // HALF):
            acc = [[jnp.zeros((8, LANES), jnp.float32) for _ in range(HALF // 8)] for _ in range(4)]
            for k in range(listed):
                for q in range(HALF // 8):
                    start = k * LANES + h * HALF + q * 8
                    g = g_buf[turn, start : start + 8, :]
                    for c in range(4):
                        acc[c][q] = acc[c][q] + g * coef[k, c]
            for c in range(4):
                for q in range(HALF // 8):
                    sums[c, h * HALF + q * 8 : h * HALF + q * 8 + 8, :] = acc[c][q]
        flat = [
            lax.dot_general(
                ones, sums[c], (((1,), (1,)), ((), ())), precision=lax.Precision.HIGHEST,
                preferred_element_type=jnp.float32,
            )[0:1]
            for c in range(4)
        ]
        here = pl.ds(pl.multiple_of(a * LANES, LANES), LANES)
        for c in range(3):
            f_ref[c, :, here] = x_v[c, :, here] * flat[0] - flat[c + 1]
        return carry

    lax.fori_loop(0, blocks, block, 0)
    loads[2].wait()


def exchange_kernel(
    domains, replicas, send_ref, target_h, sigma_h, mean_ref, ret_ref,
    target_ref, sigma_ref, loads, got, acc, part, back, land, out_send, out_recv, rep_send, rep_recv, back_send, back_recv,
):
    me_d = lax.axis_index("dom")
    me_r = lax.axis_index("rep")
    owned = target_ref.shape[0]
    stages = replicas.bit_length() - 1
    partners = []
    for t in range(stages):
        bit = 1 << t
        partners.append(me_r + bit - 2 * bit * lax.rem(lax.div(me_r, bit), 2))
    fetches = [
        pltpu.make_async_copy(target_h, target_ref, loads.at[0]),
        pltpu.make_async_copy(sigma_h, sigma_ref, loads.at[1]),
    ]
    for fetch in fetches:
        fetch.start()
    barrier = pltpu.get_barrier_semaphore()
    for s in range(1, domains):
        pl.semaphore_signal(
            barrier, inc=1, device_id=(me_r, lax.rem(me_d + s, domains)), device_id_type=MESH
        )
    for t in range(stages):
        pl.semaphore_signal(barrier, inc=1, device_id=(partners[t], me_d), device_id_type=MESH)
    pl.semaphore_wait(barrier, domains - 1 + stages)

    outs = [None]
    for s in range(1, domains):
        peer = lax.rem(me_d + s, domains)
        copy = pltpu.make_async_remote_copy(
            src_ref=send_ref.at[peer],
            dst_ref=got.at[s],
            send_sem=out_send.at[s],
            recv_sem=out_recv.at[s],
            device_id=(me_r, peer),
            device_id_type=MESH,
        )
        copy.start()
        outs.append(copy)

    row = lax.broadcasted_iota(jnp.int32, (owned, CAPACITY), 0).astype(jnp.float32)

    def picks_of(s):
        slots = (
            send_ref[me_d, CAPACITY : CAPACITY + 1, :] if s == 0 else got[s, CAPACITY : CAPACITY + 1, :]
        )
        return jnp.where(row == slots[:, :CAPACITY], 1.0, 0.0).astype(jnp.bfloat16)

    total = jnp.zeros((owned, LANES), jnp.float32)
    for s in range(domains):
        if s:
            outs[s].wait_recv()
        rows = send_ref[me_d, :CAPACITY, :] if s == 0 else got[s, :CAPACITY, :]
        picks = picks_of(s)
        for piece in three(rows):
            total = total + jnp.dot(picks, piece, preferred_element_type=jnp.float32)
    acc[0] = total
    swaps = []
    for t in range(stages):
        copy = pltpu.make_async_remote_copy(
            src_ref=acc.at[t],
            dst_ref=part.at[t],
            send_sem=rep_send.at[t],
            recv_sem=rep_recv.at[t],
            device_id=(partners[t], me_d),
            device_id_type=MESH,
        )
        copy.start()
        swaps.append(copy)
        copy.wait_recv()
        total = total + part[t]
        if t + 1 < stages:
            acc[t + 1] = total
    mean = total / replicas
    mean_ref[...] = mean
    for fetch in fetches:
        fetch.wait()
    misfit = mean - target_ref[...]
    sigmas = sigma_ref[...]
    adjoint = misfit / (sigmas * sigmas + 0.5 * misfit * misfit) / replicas
    pieces = three(adjoint)
    backs = []
    for s in list(range(1, domains)) + [0]:
        picks = picks_of(s)
        rows = jnp.zeros((CAPACITY, LANES), jnp.float32)
        for piece in pieces:
            rows = rows + lax.dot_general(
                picks, piece, (((0,), (0,)), ((), ())), preferred_element_type=jnp.float32
            )
        if s == 0:
            ret_ref[me_d] = rows
            continue
        back[s] = rows
        peer = lax.rem(me_d + domains - s, domains)
        copy = pltpu.make_async_remote_copy(
            src_ref=back.at[s],
            dst_ref=land.at[s],
            send_sem=back_send.at[s],
            recv_sem=back_recv.at[s],
            device_id=(me_r, peer),
            device_id_type=MESH,
        )
        copy.start()
        backs.append((s, copy))
    for s, copy in backs:
        copy.wait_recv()
        ret_ref[lax.rem(me_d + s, domains)] = land[s]
    for copy in outs[1:] + swaps + [copy for _, copy in backs]:
        copy.wait_send()


def shards(
    coords, atom_var, atom_weight, atoms_live, block_list, owner_map,
    comp_means, comp_var, comp_weight, target, noise_sigma,
):
    replicas = lax.axis_size("rep")
    domains = lax.axis_size("dom")
    blocks, listed = block_list.shape
    comp_blocks = owner_map.shape[0]
    owned = target.shape[0] // LANES
    entries = blocks * listed
    x = coords.transpose(1, 0, 2)
    lst = block_list.reshape(-1)
    cv = comp_var.reshape(comp_blocks, LANES)
    cw = comp_weight.reshape(comp_blocks, LANES)
    f32, i32 = jnp.float32, jnp.int32
    whole = pl.BlockSpec(memory_space=VMEM)
    far = pl.BlockSpec(memory_space=pltpu.HBM)
    send, pos, table, g = pl.pallas_call(
        functools.partial(pair_kernel, listed, owned),
        in_specs=[far] * 9,
        out_specs=[whole, pl.BlockSpec(memory_space=pltpu.SMEM), whole, far],
        out_shape=[
            jax.ShapeDtypeStruct((domains, ROWS, LANES), f32),
            jax.ShapeDtypeStruct((entries,), i32),
            jax.ShapeDtypeStruct((entries, 4, LANES), f32),
            jax.ShapeDtypeStruct((blocks, listed * LANES, LANES), f32),
        ],
        scratch_shapes=[
            VMEM((OUT_SLOTS, listed * LANES, LANES), f32),
            pltpu.SemaphoreType.DMA((OUT_SLOTS,)),
            pltpu.SMEM((blocks,), i32),
            pltpu.SMEM((entries,), i32),
            pltpu.SMEM((comp_blocks,), i32),
            VMEM(x.shape, f32),
            VMEM((blocks, LANES), f32),
            VMEM((blocks, LANES), f32),
            VMEM(comp_means.shape, f32),
            VMEM(cv.shape, f32),
            VMEM(cw.shape, f32),
            pltpu.SMEM((domains,), i32),
            VMEM((LANES, LANES), f32),
            VMEM((LANES, LANES), f32),
            pltpu.SemaphoreType.DMA((9,)),
        ],
        compiler_params=pltpu.CompilerParams(vmem_limit_bytes=57 << 20),
        name="pairs",
    )(
        atoms_live, lst, owner_map, x,
        atom_var.reshape(blocks, LANES), atom_weight.reshape(blocks, LANES),
        comp_means, cv, cw,
    )
    stages = replicas.bit_length() - 1
    mean, ret = pl.pallas_call(
        functools.partial(exchange_kernel, domains, replicas),
        in_specs=[whole, far, far],
        out_specs=[whole] * 2,
        out_shape=[
            jax.ShapeDtypeStruct((owned, LANES), f32),
            jax.ShapeDtypeStruct((domains, CAPACITY, LANES), f32),
        ],
        scratch_shapes=[
            VMEM((owned, LANES), f32),
            VMEM((owned, LANES), f32),
            pltpu.SemaphoreType.DMA((2,)),
            VMEM((domains, ROWS, LANES), f32),
            VMEM((stages, owned, LANES), f32),
            VMEM((stages, owned, LANES), f32),
            VMEM((domains, CAPACITY, LANES), f32),
            VMEM((domains, CAPACITY, LANES), f32),
            pltpu.SemaphoreType.DMA((domains,)),
            pltpu.SemaphoreType.DMA((domains,)),
            pltpu.SemaphoreType.DMA((stages,)),
            pltpu.SemaphoreType.DMA((stages,)),
            pltpu.SemaphoreType.DMA((domains,)),
            pltpu.SemaphoreType.DMA((domains,)),
        ],
        compiler_params=pltpu.CompilerParams(
            collective_id=0, has_side_effects=True, vmem_limit_bytes=57 << 20
        ),
        name="exchange",
    )(send, target.reshape(owned, LANES), noise_sigma.reshape(owned, LANES))
    forces, mean = pl.pallas_call(
        functools.partial(force_kernel, listed),
        in_specs=[pl.BlockSpec(memory_space=pl.ANY), far, far, whole, whole, whole],
        out_specs=[whole, far],
        out_shape=[
            jax.ShapeDtypeStruct(x.shape, f32),
            jax.ShapeDtypeStruct((owned, LANES), f32),
        ],
        scratch_shapes=[
            VMEM((IN_SLOTS, listed * LANES, LANES), f32),
            pltpu.SemaphoreType.DMA((IN_SLOTS,)),
            pltpu.SMEM((entries,), i32),
            VMEM(x.shape, f32),
            VMEM((listed, 4, 8, LANES), f32),
            VMEM((4, LANES, LANES), f32),
            pltpu.SemaphoreType.DMA((3,)),
        ],
        compiler_params=pltpu.CompilerParams(vmem_limit_bytes=57 << 20),
        name="forces",
    )(pos, x, g, ret.reshape(domains * CAPACITY, LANES), table, mean)
    return (mean.reshape(-1), forces.transpose(1, 0, 2))


def solution(mesh):
    return jax.shard_map(
        shards,
        mesh=mesh,
        in_specs=(
            P("rep", None, "dom"),
            P("dom"),
            P("dom"),
            P("dom"),
            P("dom", None),
            P(),
            P(),
            P(),
            P(),
            P("dom"),
            P("dom"),
        ),
        out_specs=(P("dom"), P("rep", None, "dom")),
        check_vma=False,
    )
```
